256 devices in a mesh: row: 8 (over y, core), col: 32 (over z, x).
Axes of the slice: x: 4, y: 4, z: 8, core: 2. Of those that a mesh axis runs over, the one named last changes fastest.
Arguments:
- diag_block: float32 [1024, 1024], P('row')
- panel: bfloat16 [64, 1024, 1024], P('col', 'row'), may hold values from -1 to 1
- trailing: bfloat16 [32, 12, 1024, 1024], P('col', None, 'row'), may hold values from -6 to 6
- slot_rows: int32 [32, 12], replicated, may hold values from -1 to 63, as said below
- slot_cols: int32 [32, 12], replicated, may hold values from 0 to 1, as said below
Outputs:
- panel_factor: bfloat16 [64, 1024, 1024], P('col', 'row')
- updated: bfloat16 [32, 12, 1024, 1024], P('col', None, 'row')
The draws below stay inside these ranges and needn't reach their ends.
Inputs may be any that keep to these rules, and one draw needn't show every extreme that they name: Slot s of grid column c holds the tile at tile row slot_rows[c, s] and tile column 2 * c + slot_cols[c, s] of the trailing matrix, or nothing where slot_rows[c, s] is -1. Live slots come first in each column; the pairs of one column are distinct and lie on or below the diagonal (tile row at least tile column). Within one grid column, live slots whose tile rows a and a' have a // 2 == a' // 2 have a == a'. Every column holds at least one live slot, column 0 fills all 12 slots and column 16 holds exactly one. `slot_cols`: 0 in empty slots.
All inputs are finite; a program needn't handle non-finite values.
Results may differ from the reference program's by a relative error of at most 0.0019.
Values may be sent and summed in bfloat16 or wider, within the bound.
No kernel may reach another device: no remote copies, remote signals or barrier semaphores. Data moves between devices by JAX's collectives and lax.ppermute only.
A program may use at most 128 MiB of HBM per device.

```python
import math
import jax
import jax.numpy as jnp
from jax import lax

TILE = 1024
PAN_COL = 2
SLOTS = 12
PANEL = 64
N_COL = 32


def compact_kernel(point_key):
    steps = jax.random.uniform(point_key, (TILE,), jnp.float32, 0.5, 1.5)
    points = jnp.cumsum(steps) / jnp.sum(steps)
    neighbours = min(64, TILE // 2)
    radius = neighbours / (2.0 * TILE)
    ratio = jnp.abs(points[:, None] - points[None, :]) / radius
    remain = jnp.maximum(1.0 - ratio, 0.0)
    squared = remain * remain
    return squared * squared * (4.0 * ratio + 1.0)


def draw_diag_block(key, part):
    first_key = jax.random.fold_in(jax.random.fold_in(key, 11), 0)
    second_key = jax.random.fold_in(jax.random.fold_in(key, 11), 1)
    fourth_key = jax.random.fold_in(jax.random.fold_in(key, 11), 3)
    basis = jax.random.normal(first_key, (TILE, TILE), jnp.float32) / math.sqrt(TILE)
    gram_part = 0.5 * jnp.dot(basis, basis.T, precision=lax.Precision.HIGHEST)
    extra_diag = jax.random.uniform(second_key, (TILE,), jnp.float32, 0.5, 1.5)
    matrix = compact_kernel(fourth_key) + gram_part + jnp.diag(extra_diag)
    return matrix


def slot_pattern(key):

    def one_column(col_index):
        column_key = jax.random.fold_in(jax.random.fold_in(key, 7), col_index)
        first_key, second_key, third_key = jax.random.split(column_key, 3)
        owners = jnp.arange(N_COL, dtype=jnp.int32)
        chosen_rows = owners * PAN_COL + jax.random.randint(third_key, (N_COL,), 0, PAN_COL, dtype=jnp.int32)
        candidate = jnp.arange(N_COL * PAN_COL, dtype=jnp.int32)
        owner_of = candidate // PAN_COL
        local_col = candidate % PAN_COL
        tile_row = chosen_rows[owner_of]
        allowed = (owner_of >= col_index) & (tile_row >= col_index * PAN_COL + local_col)
        scores = jax.random.randint(first_key, (N_COL * PAN_COL,), 0, 1 << 20, dtype=jnp.int32) * (N_COL * PAN_COL) + candidate
        scores = jnp.where(allowed, scores, (1 << 30) + candidate)
        ranked = jnp.argsort(scores, stable=True)[:SLOTS].astype(jnp.int32)
        available = jnp.sum(allowed.astype(jnp.int32))
        ceiling = jnp.minimum(available, SLOTS)
        live_count = jax.random.randint(second_key, (), 1, ceiling + 1, dtype=jnp.int32)
        live_count = jnp.where(col_index == 0, SLOTS, jnp.where(col_index == N_COL // 2, 1, live_count))
        live_mask = jnp.arange(SLOTS, dtype=jnp.int32) < live_count
        row_ids = jnp.where(live_mask, chosen_rows[ranked // PAN_COL], -1)
        col_ids = jnp.where(live_mask, ranked % PAN_COL, 0)
        return (row_ids.astype(jnp.int32), col_ids.astype(jnp.int32))
    return jax.vmap(one_column)(jnp.arange(N_COL, dtype=jnp.int32))


def draw_slot_rows(key, part):
    return slot_pattern(key)[0]


def draw_slot_cols(key, part):
    return slot_pattern(key)[1]


def steps_of(key, extent, shards, low, largest):
    def one(position, parts):
        steps = jax.random.uniform(jax.random.fold_in(jax.random.fold_in(key, 6), position), (parts,), jnp.float32, low / len(shards), largest / len(shards))
        return jnp.repeat(jnp.exp(steps), extent[position] // parts).reshape((-1,) + (1,) * (len(extent) - position - 1))

    level = one(*shards[0])
    for cut in shards[1:]:
        level = level * one(*cut)
    return level


def noise(key, dims, width, reach, shards=(), kind=jnp.bfloat16):
    entries = width * jax.random.normal(key, dims, jnp.float32)
    if shards:
        entries = entries * steps_of(key, dims, shards, -0.22, 0.18)
    return jnp.clip(entries, -reach, reach).astype(kind)


def setup_inputs(seed: int = 0) -> dict:
    key_of = jax.random.split(jax.random.key(seed), 6)
    diag_block = draw_diag_block(jax.random.fold_in(key_of[5], 71), 0)
    panel = noise(key_of[1], (PANEL, TILE, TILE), 0.18, 1.0, ((0, 32), (1, 8)))
    trailing = noise(key_of[2], (N_COL, SLOTS, TILE, TILE), 1.0, 6.0, ((0, 32), (2, 8)))
    slot_rows = draw_slot_rows(jax.random.fold_in(key_of[5], 71), 0)
    slot_cols = draw_slot_cols(jax.random.fold_in(key_of[5], 71), 0)
    return dict(diag_block=diag_block, panel=panel, trailing=trailing, slot_rows=slot_rows, slot_cols=slot_cols)


def reference(diag_block, panel, trailing, slot_rows, slot_cols):
    factor = jnp.linalg.cholesky(diag_block)
    stacked = panel.astype(jnp.float32).reshape(PANEL * TILE, TILE)
    solved = lax.linalg.triangular_solve(factor, stacked.T, left_side=True, lower=True)
    panel_factor = solved.T.reshape(PANEL, TILE, TILE).astype(jnp.bfloat16)
    widened = panel_factor.astype(jnp.float32)

    def one_column(packed):
        tile_block, row_ids, col_ids, col_index = packed
        live_mask = row_ids >= 0
        left_tiles = widened[jnp.maximum(row_ids, 0)]
        right_tiles = widened[col_index * PAN_COL + col_ids]
        update = jnp.einsum('sij,skj->sik', left_tiles, right_tiles, precision=lax.Precision.HIGHEST)
        previous = tile_block.astype(jnp.float32)
        lowered = jnp.where(live_mask[:, None, None], previous - update, previous)
        return lowered.astype(jnp.bfloat16)
    updated = lax.map(one_column, (trailing, slot_rows, slot_cols, jnp.arange(N_COL, dtype=jnp.int32)))
    return (panel_factor, updated)
```

```python
import jax
import jax.numpy as jnp
from jax import lax
from jax.experimental import pallas as pl
from jax.experimental.pallas import tpu as pltpu
from jax.sharding import PartitionSpec as P

HIGHEST = lax.Precision.HIGHEST
F32, BF16 = jnp.float32, jnp.bfloat16
B = 128


def lane_splat(x, lane):
    return jnp.broadcast_to(x[:, lane:lane + 1], (8, B))


def row_splat(x, row):
    return jnp.broadcast_to(x[row:row + 1, :], (8, B))


def tree_sum(terms):
    terms = list(terms)
    while len(terms) > 1:
        terms = [terms[i] + terms[i + 1] for i in range(0, len(terms), 2)]
    return terms[0]


def inverse_factor(block, out):
    sub = lax.broadcasted_iota(jnp.int32, (8, B), 0)
    lane = lax.broadcasted_iota(jnp.int32, (8, B), 1)
    rows = [block[8 * g:8 * g + 8, :] for g in range(16)]
    ones = [jnp.where(lane == sub + 8 * g, 1.0, 0.0).astype(F32) for g in range(16)]
    for g in range(16):
        left, right = rows[g], ones[g]
        cols = [lane_splat(left, 8 * g + k) for k in range(8)]
        done = jnp.zeros((8, B), F32)
        for k in range(8):
            here = sub == k
            pivot = row_splat(cols[k], k)
            recip = 1.0 / pivot
            right_row = row_splat(right, k)
            done = jnp.where(here, right_row * lax.rsqrt(pivot), done)
            left_row = row_splat(left, k) * recip
            right_row = right_row * recip
            for m in range(k + 1, 8):
                entry = row_splat(cols[m], k) * recip
                cols[m] = jnp.where(here, entry, cols[m] - cols[k] * entry)
            left = jnp.where(here, left_row, left - cols[k] * left_row)
            right = jnp.where(here, right_row, right - cols[k] * right_row)
        out[8 * g:8 * g + 8, :] = done
        if g < 15:
            left_rows = [row_splat(left, k) for k in range(8)]
            right_rows = [row_splat(right, k) for k in range(8)]
            for h in range(g + 1, 16):
                coefs = [lane_splat(rows[h], 8 * g + k) for k in range(8)]
                rows[h] = rows[h] - tree_sum(coefs[k] * left_rows[k] for k in range(8))
                ones[h] = ones[h] - tree_sum(coefs[k] * right_rows[k] for k in range(8))


def dot(a, b, contract, precision=None):
    return lax.dot_general(a, b, ((contract[0], contract[1]), ((), ())), precision=precision, preferred_element_type=F32)


def factor_kernel(ranks, *refs):
    parts, (high, low), (work, diag_inverse) = refs[:8], refs[8:10], refs[10:]
    for q in range(8):
        work[pl.ds(pl.multiple_of(ranks[q] * B, B), B), :] = parts[q][...]

    def step(j, carry):
        o = pl.multiple_of(j * B, B)
        inverse_factor(work[pl.ds(o, B), pl.ds(o, B)], diag_inverse)

        def update(j):
            def run():
                s, e = j * B, j * B + B
                inv = diag_inverse[...]
                if j:
                    work[s:e, :s] = dot(inv, work[s:e, :s], ((1,), (0,)), HIGHEST)
                work[s:e, s:e] = inv
                if j < 7:
                    work[s:e, e:] = dot(inv, work[s:e, e:], ((1,), (0,)), HIGHEST)
                for i in range(j + 1, 8):
                    t, u = i * B, i * B + B
                    coef = work[s:e, t:u]
                    if j:
                        work[t:u, :s] -= dot(coef, work[s:e, :s], ((0,), (0,)), HIGHEST)
                    work[t:u, s:e] = -dot(coef, work[s:e, s:e], ((0,), (0,)), HIGHEST)
                    work[t:u, t:] -= dot(coef, work[s:e, t:], ((0,), (0,)), HIGHEST)
            return run

        lax.switch(j, [update(j) for j in range(8)])
        return carry

    lax.fori_loop(0, 8, step, 0)
    for j in range(8):
        s, e = j * B, j * B + B
        whole = work[s:e, :e]
        top = whole.astype(BF16)
        high[s:e, :e] = top
        low[s:e, :e] = (whole - top.astype(F32)).astype(BF16)
        if e < 1024:
            high[s:e, e:] = jnp.zeros((B, 1024 - e), BF16)
            low[s:e, e:] = jnp.zeros((B, 1024 - e), BF16)


def inverse_parts(ranks, parts):
    vmem = pl.BlockSpec(memory_space=pltpu.VMEM)
    half = jax.ShapeDtypeStruct((1024, 1024), BF16)
    return pl.pallas_call(
        factor_kernel,
        out_shape=(half, half),
        in_specs=[pl.BlockSpec(memory_space=pltpu.SMEM)] + [vmem] * 8,
        out_specs=(vmem, vmem),
        scratch_shapes=[pltpu.VMEM((1024, 1024), F32), pltpu.VMEM((B, B), F32)],
        compiler_params=pltpu.CompilerParams(vmem_limit_bytes=40 << 20),
        cost_estimate=pl.CostEstimate(flops=20_000_000_000, bytes_accessed=100_000_000, transcendentals=0),
        name="factor",
    )(ranks, *parts)


def solve_rows(raw, high, low):
    pieces = []
    for n in range(4):
        s, e = 256 * n, 256 * n + 256
        left = raw[:, :e]
        piece = dot(left, low[s:e, :e], ((1,), (1,))) + dot(left, high[s:e, :e], ((1,), (1,)))
        pieces.append(piece.astype(BF16))
    return jnp.concatenate(pieces, axis=1)


def own_kernel(ranks, raw, high, low, out):
    solved = solve_rows(raw[...].reshape(2 * B, 1024), high, low)
    out[...] = solved.reshape(2, B, 1024)


def solve_own(ranks, raw, high, low):
    whole = pl.BlockSpec((1024, 1024), lambda q, r: (0, 0))
    return pl.pallas_call(
        own_kernel,
        out_shape=jax.ShapeDtypeStruct((2, 1024, 1024), BF16),
        grid_spec=pltpu.PrefetchScalarGridSpec(
            num_scalar_prefetch=1,
            grid=(8,),
            in_specs=[pl.BlockSpec((None, 2, B, 1024), lambda q, r: (q, 0, 0, 0)), whole, whole],
            out_specs=pl.BlockSpec((2, B, 1024), lambda q, r: (0, r[q], 0)),
        ),
        compiler_params=pltpu.CompilerParams(vmem_limit_bytes=32 << 20),
        cost_estimate=pl.CostEstimate(flops=6_000_000_000, bytes_accessed=12_000_000, transcendentals=0),
        name="own",
    )(ranks, raw, high, low)


def slot_kernel(table, raw, high, low, tiles, trailing, out):
    s = pl.program_id(0)

    @pl.when(table[2, s] > 0)
    def _():
        left = solve_rows(raw[...], high, low)
        product = dot(left, tiles[table[1, s]], ((1,), (1,)))
        out[...] = (trailing[...].astype(F32) - product).astype(BF16)

    @pl.when(table[2, s] == 0)
    def _():
        out[...] = trailing[...]


def update_slots(table, slices, high, low, tiles, trailing):
    whole = pl.BlockSpec((1024, 1024), lambda s, t: (0, 0))
    slot = pl.BlockSpec((None, B, 1024), lambda s, t: (s, 0, 0))
    return pl.pallas_call(
        slot_kernel,
        out_shape=jax.ShapeDtypeStruct((12, B, 1024), BF16),
        grid_spec=pltpu.PrefetchScalarGridSpec(
            num_scalar_prefetch=1,
            grid=(12,),
            in_specs=[
                pl.BlockSpec((None, B, 1024), lambda s, t: (t[0, s], 0, 0)),
                whole,
                whole,
                pl.BlockSpec((2, 1024, 1024), lambda s, t: (0, 0, 0)),
                slot,
            ],
            out_specs=slot,
        ),
        compiler_params=pltpu.CompilerParams(vmem_limit_bytes=40 << 20),
        cost_estimate=pl.CostEstimate(flops=8_000_000_000, bytes_accessed=18_000_000, transcendentals=0),
        name="slots",
    )(table, slices, high, low, tiles, trailing)


def shift_y(x, k):
    return lax.ppermute(x, "row", [(r, (r + 2 * k) % 8) for r in range(8)])


def other_core(x):
    return lax.ppermute(x, "row", [(r, r ^ 1) for r in range(8)])


def row_parts(x):
    same = [x, shift_y(x, 1), shift_y(x, 3), shift_y(x, 2)]
    return same + [other_core(p) for p in same]


def local(diag_block, panel, trailing, slot_rows, slot_cols):
    row, col = lax.axis_index("row"), lax.axis_index("col")
    shifts = jnp.array([0, 1, 3, 2], jnp.int32)
    ranks = jnp.concatenate([(row - 2 * shifts) % 8, ((row ^ 1) - 2 * shifts) % 8]).astype(jnp.int32)
    wanted = jnp.any(slot_rows.reshape(1, -1) == jnp.arange(64, dtype=jnp.int32)[:, None], axis=1).reshape(32, 2)
    both = wanted[:, 0] & wanted[:, 1]
    first = jnp.where(wanted[:, 0], 0, 1)
    mine = lax.dynamic_index_in_dim(panel, first[col], 0, keepdims=False)
    slices = lax.all_gather(mine, "col", axis=0, tiled=False)

    high, low = inverse_parts(ranks, row_parts(diag_block))
    tiles = solve_own(ranks, jnp.stack(row_parts(panel)), high, low)
    panel_factor = lax.dynamic_slice_in_dim(tiles, row * B, B, axis=1)

    rows = lax.dynamic_index_in_dim(slot_rows, col, 0, keepdims=False)
    cols = lax.dynamic_index_in_dim(slot_cols, col, 0, keepdims=False)
    live = rows >= 0
    owner = jnp.maximum(rows, 0) // 2
    second = both[owner] & (rows % 2 == 1)
    table = jnp.stack([owner + 32 * (second & live), cols, live.astype(jnp.int32)])

    def one_tile(slices):
        return update_slots(table, slices, high, low, tiles, trailing[0])

    def two_tiles(slices):
        more = lax.all_gather(panel[1], "col", axis=0, tiled=False)
        return update_slots(table, jnp.concatenate([slices, more]), high, low, tiles, trailing[0])

    updated = lax.cond(jnp.any(both), two_tiles, one_tile, slices)
    return (panel_factor, updated[None])


def solution(mesh):
    return jax.shard_map(
        local,
        mesh=mesh,
        in_specs=(P("row", None), P("col", "row", None), P("col", None, "row", None), P(), P()),
        out_specs=(P("col", "row", None), P("col", None, "row", None)),
        check_vma=False,
    )
```

```python
import jax
import jax.numpy as jnp
from jax import lax
from jax.experimental import pallas as pl
from jax.experimental.pallas import tpu as pltpu
from jax.sharding import PartitionSpec as P

HIGHEST = lax.Precision.HIGHEST
F32, BF16 = jnp.float32, jnp.bfloat16
B = 128


def lane_splat(x, lane):
    return jnp.broadcast_to(x[:, lane:lane + 1], (8, B))


def row_splat(x, row):
    return jnp.broadcast_to(x[row:row + 1, :], (8, B))


def tree_sum(terms):
    terms = list(terms)
    while len(terms) > 1:
        terms = [terms[i] + terms[i + 1] for i in range(0, len(terms), 2)]
    return terms[0]


def inverse_factor(block, out):
    sub = lax.broadcasted_iota(jnp.int32, (8, B), 0)
    lane = lax.broadcasted_iota(jnp.int32, (8, B), 1)
    rows = [block[8 * g:8 * g + 8, :] for g in range(16)]
    ones = [jnp.where(lane == sub + 8 * g, 1.0, 0.0).astype(F32) for g in range(16)]
    for g in range(16):
        left, right = rows[g], ones[g]
        cols = [lane_splat(left, 8 * g + k) for k in range(8)]
        done = jnp.zeros((8, B), F32)
        for k in range(8):
            here = sub == k
            pivot = row_splat(cols[k], k)
            recip = 1.0 / pivot
            right_row = row_splat(right, k)
            done = jnp.where(here, right_row * lax.rsqrt(pivot), done)
            left_row = row_splat(left, k) * recip
            right_row = right_row * recip
            for m in range(k + 1, 8):
                entry = row_splat(cols[m], k) * recip
                cols[m] = jnp.where(here, entry, cols[m] - cols[k] * entry)
            left = jnp.where(here, left_row, left - cols[k] * left_row)
            right = jnp.where(here, right_row, right - cols[k] * right_row)
        out[8 * g:8 * g + 8, :] = done
        if g < 15:
            left_rows = [row_splat(left, k) for k in range(8)]
            right_rows = [row_splat(right, k) for k in range(8)]
            for h in range(g + 1, 16):
                coefs = [lane_splat(rows[h], 8 * g + k) for k in range(8)]
                rows[h] = rows[h] - tree_sum(coefs[k] * left_rows[k] for k in range(8))
                ones[h] = ones[h] - tree_sum(coefs[k] * right_rows[k] for k in range(8))


def dot(a, b, contract, precision=None):
    return lax.dot_general(a, b, ((contract[0], contract[1]), ((), ())), precision=precision, preferred_element_type=F32)


def factor_kernel(ranks, *refs):
    parts, (high, low), (work, diag_inverse) = refs[:8], refs[8:10], refs[10:]
    for q in range(8):
        work[pl.ds(pl.multiple_of(ranks[q] * B, B), B), :] = parts[q][...]

    def step(j, carry):
        o = pl.multiple_of(j * B, B)
        inverse_factor(work[pl.ds(o, B), pl.ds(o, B)], diag_inverse)

        def update(j):
            def run():
                s, e = j * B, j * B + B
                inv = diag_inverse[...]
                if j:
                    work[s:e, :s] = dot(inv, work[s:e, :s], ((1,), (0,)), HIGHEST)
                work[s:e, s:e] = inv
                if j < 7:
                    work[s:e, e:] = dot(inv, work[s:e, e:], ((1,), (0,)), HIGHEST)
                for i in range(j + 1, 8):
                    t, u = i * B, i * B + B
                    coef = work[s:e, t:u]
                    if j:
                        work[t:u, :s] -= dot(coef, work[s:e, :s], ((0,), (0,)), HIGHEST)
                    work[t:u, s:e] = -dot(coef, work[s:e, s:e], ((0,), (0,)), HIGHEST)
                    work[t:u, t:] -= dot(coef, work[s:e, t:], ((0,), (0,)), HIGHEST)
            return run

        lax.switch(j, [update(j) for j in range(8)])
        return carry

    lax.fori_loop(0, 8, step, 0)
    for j in range(8):
        s, e = j * B, j * B + B
        whole = work[s:e, :e]
        top = whole.astype(BF16)
        high[s:e, :e] = top
        low[s:e, :e] = (whole - top.astype(F32)).astype(BF16)
        if e < 1024:
            high[s:e, e:] = jnp.zeros((B, 1024 - e), BF16)
            low[s:e, e:] = jnp.zeros((B, 1024 - e), BF16)


def inverse_parts(ranks, parts):
    vmem = pl.BlockSpec(memory_space=pltpu.VMEM)
    half = jax.ShapeDtypeStruct((1024, 1024), BF16)
    return pl.pallas_call(
        factor_kernel,
        out_shape=(half, half),
        in_specs=[pl.BlockSpec(memory_space=pltpu.SMEM)] + [vmem] * 8,
        out_specs=(vmem, vmem),
        scratch_shapes=[pltpu.VMEM((1024, 1024), F32), pltpu.VMEM((B, B), F32)],
        compiler_params=pltpu.CompilerParams(vmem_limit_bytes=16 << 20),
        cost_estimate=pl.CostEstimate(flops=20_000_000_000, bytes_accessed=100_000_000, transcendentals=0),
        name="factor",
    )(ranks, *parts)


def solve_rows(raw, high, low):
    pieces = []
    for n in range(4):
        s, e = 256 * n, 256 * n + 256
        left = raw[:, :e]
        piece = dot(left, low[s:e, :e], ((1,), (1,))) + dot(left, high[s:e, :e], ((1,), (1,)))
        pieces.append(piece.astype(BF16))
    return jnp.concatenate(pieces, axis=1)


def own_kernel(ranks, *refs):
    parts, (high, low, tiles, mine) = refs[:8], refs[8:]
    for q in range(8):
        solved = solve_rows(parts[q][...].reshape(2 * B, 1024), high, low).reshape(2, B, 1024)
        tiles[:, pl.ds(pl.multiple_of(ranks[q] * B, B), B), :] = solved
        if q == 0:
            mine[...] = solved


def solve_own(ranks, parts, high, low):
    vmem = pl.BlockSpec(memory_space=pltpu.VMEM)
    return pl.pallas_call(
        own_kernel,
        out_shape=(jax.ShapeDtypeStruct((2, 1024, 1024), BF16), jax.ShapeDtypeStruct((2, B, 1024), BF16)),
        in_specs=[pl.BlockSpec(memory_space=pltpu.SMEM)] + [vmem] * 10,
        out_specs=(vmem, vmem),
        compiler_params=pltpu.CompilerParams(vmem_limit_bytes=8 << 20),
        cost_estimate=pl.CostEstimate(flops=6_000_000_000, bytes_accessed=12_000_000, transcendentals=0),
        name="own",
    )(ranks, *parts, high, low)


def slot_kernel(table, source, high, low, tiles, trailing, out, raw, new, left, in_sems, out_sems):
    def rows(p):
        return pl.ds(pl.multiple_of(p * B, B), B)

    def raw_copy(p):
        return pltpu.make_async_copy(source.at[table[1, p]], raw.at[rows(p)], in_sems.at[p])

    def new_copy(p):
        return pltpu.make_async_copy(new.at[rows(p)], out.at[table[0, p]], out_sems.at[p])

    def subtract(p, first, b):
        for n in range(0, 1024, 256):
            product = dot(left[first * B:, :], tiles[b, n:n + 256, :], ((1,), (1,)))
            for i in range(2 - first):
                before = trailing[table[0, p + i], :, n:n + 256].astype(F32)
                new[rows(p + i), n:n + 256] = (before - product[i * B:i * B + B, :]).astype(BF16)

    for p in range(12):
        raw_copy(p).start()

    def pair(c, carry):
        p = 2 * c
        raw_copy(p).wait()
        raw_copy(p + 1).wait()
        live, both = table[3, p] > 0, table[3, p + 1] > 0

        @pl.when(live)
        def _():
            block = pl.ds(pl.multiple_of(p * B, 2 * B), 2 * B)
            for n in range(0, 1024, 256):
                e = n + 256
                some = raw[block, :e]
                piece = dot(some, low[n:e, :e], ((1,), (1,))) + dot(some, high[n:e, :e], ((1,), (1,)))
                left[:, n:e] = piece.astype(BF16)
            subtract(p, 0, table[2, p])

        @pl.when(jnp.logical_and(both, table[2, p + 1] != table[2, p]))
        def _():
            subtract(p + 1, 1, table[2, p + 1])

        for i, used in enumerate((live, both)):
            @pl.when(jnp.logical_not(used))
            def _():
                new[rows(p + i), :] = trailing[table[0, p + i]]

            new_copy(p + i).start()
        return carry

    lax.fori_loop(0, 6, pair, 0)
    for p in range(12):
        new_copy(p).wait()


def update_slots(table, source, high, low, tiles, trailing):
    vmem, hbm = pl.BlockSpec(memory_space=pltpu.VMEM), pl.BlockSpec(memory_space=pltpu.HBM)
    return pl.pallas_call(
        slot_kernel,
        out_shape=jax.ShapeDtypeStruct((12, B, 1024), BF16),
        in_specs=[pl.BlockSpec(memory_space=pltpu.SMEM), hbm, vmem, vmem, vmem, vmem],
        out_specs=hbm,
        scratch_shapes=[pltpu.VMEM((12 * B, 1024), BF16)] * 2
        + [pltpu.VMEM((2 * B, 1024), BF16), pltpu.SemaphoreType.DMA((12,)), pltpu.SemaphoreType.DMA((12,))],
        compiler_params=pltpu.CompilerParams(vmem_limit_bytes=38 << 20),
        cost_estimate=pl.CostEstimate(flops=8_000_000_000, bytes_accessed=12_000_000, transcendentals=0),
        name="slots",
    )(table, source, high, low, tiles, trailing)


def shift_y(x, k):
    return lax.ppermute(x, "row", [(r, (r + 2 * k) % 8) for r in range(8)])


def other_core(x):
    return lax.ppermute(x, "row", [(r, r ^ 1) for r in range(8)])


def row_parts(x):
    same = [x, shift_y(x, 1), shift_y(x, 3), shift_y(x, 2)]
    return same + [other_core(p) for p in same]


def local(diag_block, panel, trailing, slot_rows, slot_cols):
    row, col = lax.axis_index("row"), lax.axis_index("col")
    order = jnp.array([0, 1, 3, 2], jnp.int32)
    ranks = jnp.concatenate([(row - 2 * order) % 8, ((row ^ 1) - 2 * order) % 8]).astype(jnp.int32)

    source = lax.all_gather(panel, "col", axis=0, tiled=True)
    diag_parts = row_parts(diag_block)
    own, *diag_parts = lax.optimization_barrier((panel, *diag_parts))
    own_parts = row_parts(own)
    high, low = inverse_parts(ranks, diag_parts)

    tiles, panel_factor = solve_own(ranks, own_parts, high, low)

    rows = lax.dynamic_index_in_dim(slot_rows, col, 0, keepdims=False)
    cols = lax.dynamic_index_in_dim(slot_cols, col, 0, keepdims=False)
    live = rows >= 0
    key = jnp.where(live, cols, 2)
    slot = jnp.arange(12, dtype=jnp.int32)
    before = (key[None, :] < key[:, None]) | ((key[None, :] == key[:, None]) & (slot[None, :] < slot[:, None]))
    place = jnp.sum(before.astype(jnp.int32), axis=1)
    fields = jnp.stack([slot, jnp.maximum(rows, 0), cols, live.astype(jnp.int32)])
    chosen = (place[None, :] == slot[:, None]).astype(jnp.int32)
    table = jnp.sum(fields[:, None, :] * chosen[None, :, :], axis=2)

    updated = update_slots(table, source, high, low, tiles, trailing[0])
    return (panel_factor, updated[None])


def solution(mesh):
    return jax.shard_map(
        local,
        mesh=mesh,
        in_specs=(P("row", None), P("col", "row", None), P("col", None, "row", None), P(), P()),
        out_specs=(P("col", "row", None), P("col", None, "row", None)),
        check_vma=False,
    )
```

```python
import functools

import jax
import jax.numpy as jnp
from jax import lax
from jax.experimental import pallas as pl
from jax.experimental.pallas import tpu as pltpu
from jax.sharding import PartitionSpec as P

HIGHEST = lax.Precision.HIGHEST
F32, BF16 = jnp.float32, jnp.bfloat16
B = 128
SPLIT = 1
A_ROWS = 80
ORDER = (0, 1, 3, 2)


def lane_splat(x, lane):
    return jnp.broadcast_to(x[:, lane:lane + 1], (8, B))


def row_splat(x, row):
    return jnp.broadcast_to(x[row:row + 1, :], (8, B))


def tree_sum(terms):
    terms = list(terms)
    while len(terms) > 1:
        terms = [terms[i] + terms[i + 1] for i in range(0, len(terms), 2)]
    return terms[0]


def inverse_factor(block, out):
    sub = lax.broadcasted_iota(jnp.int32, (8, B), 0)
    lane = lax.broadcasted_iota(jnp.int32, (8, B), 1)
    rows = [block[8 * g:8 * g + 8, :] for g in range(16)]
    ones = [jnp.where(lane == sub + 8 * g, 1.0, 0.0).astype(F32) for g in range(16)]
    for g in range(16):
        left, right = rows[g], ones[g]
        cols = [lane_splat(left, 8 * g + k) for k in range(8)]
        done = jnp.zeros((8, B), F32)
        for k in range(8):
            here = sub == k
            pivot = row_splat(cols[k], k)
            recip = 1.0 / pivot
            right_row = row_splat(right, k)
            done = jnp.where(here, right_row * lax.rsqrt(pivot), done)
            left_row = row_splat(left, k) * recip
            right_row = right_row * recip
            for m in range(k + 1, 8):
                entry = row_splat(cols[m], k) * recip
                cols[m] = jnp.where(here, entry, cols[m] - cols[k] * entry)
            left = jnp.where(here, left_row, left - cols[k] * left_row)
            right = jnp.where(here, right_row, right - cols[k] * right_row)
        out[8 * g:8 * g + 8, :] = done
        if g < 15:
            left_rows = [row_splat(left, k) for k in range(8)]
            right_rows = [row_splat(right, k) for k in range(8)]
            for h in range(g + 1, 16):
                coefs = [lane_splat(rows[h], 8 * g + k) for k in range(8)]
                rows[h] = rows[h] - tree_sum(coefs[k] * left_rows[k] for k in range(8))
                ones[h] = ones[h] - tree_sum(coefs[k] * right_rows[k] for k in range(8))


def dot(a, b, contract, precision=None):
    return lax.dot_general(a, b, ((contract[0], contract[1]), ((), ())), precision=precision, preferred_element_type=F32)


def clear_below(work, inv, j):
    s, e = j * B, j * B + B
    if j:
        work[s:e, :s] = dot(inv, work[s:e, :s], ((1,), (0,)), HIGHEST)
    work[s:e, s:e] = inv
    if j < 7:
        work[s:e, e:] = dot(inv, work[s:e, e:], ((1,), (0,)), HIGHEST)
    for t in range(e, 1024, B):
        coef = work[s:e, t:t + B]
        if j:
            work[t:t + B, :s] -= dot(coef, work[s:e, :s], ((0,), (0,)), HIGHEST)
        work[t:t + B, s:e] = -dot(coef, inv, ((0,), (0,)), HIGHEST)
        work[t:t + B, t:] -= dot(coef, work[s:e, t:], ((0,), (0,)), HIGHEST)


def eliminate(work, diag_inverse, first, last):
    def step(j, carry):
        here = pl.ds(pl.multiple_of(j * B, B), B)
        inverse_factor(work[here, here], diag_inverse)
        branches = [functools.partial(clear_below, work, diag_inverse[...], k) for k in range(first, last)]
        lax.switch(j - first, branches)
        return carry

    lax.fori_loop(first, last, step, 0)


def first_kernel(ranks, *refs):
    parts, work, diag_inverse = refs[:8], refs[8], refs[9]
    for q in range(8):
        work[pl.ds(pl.multiple_of(ranks[q] * B, B), B), :] = parts[q][...]
    eliminate(work, diag_inverse, 0, SPLIT)


def second_kernel(start, work, high, low, diag_inverse):
    eliminate(work, diag_inverse, SPLIT, 8)
    for j in range(8):
        s, e = j * B, j * B + B
        whole = work[s:e, :e]
        top = whole.astype(BF16)
        high[s:e, :e] = top
        low[s:e, :e] = (whole - top.astype(F32)).astype(BF16)
        if e < 1024:
            high[s:e, e:] = jnp.zeros((B, 1024 - e), BF16)
            low[s:e, e:] = jnp.zeros((B, 1024 - e), BF16)


def first_blocks(ranks, parts):
    vmem = pl.BlockSpec(memory_space=pltpu.VMEM)
    return pl.pallas_call(
        first_kernel,
        out_shape=jax.ShapeDtypeStruct((1024, 1024), F32),
        in_specs=[pl.BlockSpec(memory_space=pltpu.SMEM)] + [vmem] * 8,
        out_specs=vmem,
        scratch_shapes=[pltpu.VMEM((B, B), F32)],
        compiler_params=pltpu.CompilerParams(vmem_limit_bytes=8 << 20),
        cost_estimate=pl.CostEstimate(flops=20_000_000_000, bytes_accessed=50_000_000, transcendentals=0),
        name="first",
    )(ranks, *parts)


def inverse_parts(work):
    vmem = pl.BlockSpec(memory_space=pltpu.VMEM)
    half = jax.ShapeDtypeStruct((1024, 1024), BF16)
    _, high, low = pl.pallas_call(
        second_kernel,
        out_shape=(jax.ShapeDtypeStruct((1024, 1024), F32), half, half),
        in_specs=[vmem],
        out_specs=(vmem, vmem, vmem),
        scratch_shapes=[pltpu.VMEM((B, B), F32)],
        input_output_aliases={0: 0},
        compiler_params=pltpu.CompilerParams(vmem_limit_bytes=8 << 20),
        cost_estimate=pl.CostEstimate(flops=20_000_000_000, bytes_accessed=50_000_000, transcendentals=0),
        name="second",
    )(work)
    return high, low


def solve_rows(raw, high, low):
    pieces = []
    for n in range(4):
        s, e = 256 * n, 256 * n + 256
        left = raw[:, :e]
        piece = dot(left, low[s:e, :e], ((1,), (1,))) + dot(left, high[s:e, :e], ((1,), (1,)))
        pieces.append(piece.astype(BF16))
    return jnp.concatenate(pieces, axis=1)


def own_kernel(ranks, *refs):
    parts, (high, low, tiles, mine) = refs[:8], refs[8:]
    for q in range(8):
        solved = solve_rows(parts[q][...].reshape(2 * B, 1024), high, low).reshape(2, B, 1024)
        tiles[:, pl.ds(pl.multiple_of(ranks[q] * B, B), B), :] = solved
        if q == 0:
            mine[...] = solved


def solve_own(ranks, parts, high, low):
    vmem = pl.BlockSpec(memory_space=pltpu.VMEM)
    return pl.pallas_call(
        own_kernel,
        out_shape=(jax.ShapeDtypeStruct((2, 1024, 1024), BF16), jax.ShapeDtypeStruct((2, B, 1024), BF16)),
        in_specs=[pl.BlockSpec(memory_space=pltpu.SMEM)] + [vmem] * 10,
        out_specs=(vmem, vmem),
        compiler_params=pltpu.CompilerParams(vmem_limit_bytes=8 << 20),
        cost_estimate=pl.CostEstimate(flops=1000, bytes_accessed=1000, transcendentals=0),
        name="own",
    )(ranks, *parts, high, low)


def slot_kernel(table, here, r1, r2, r3, deep, high_in, low_in, tiles_in, trailing_in, out, *scratch):
    high, low, tiles, raw, old, new, left, in_sems, out_sems, sems = scratch
    ring = (r1, r2, r3)

    def rows(p):
        return pl.ds(pl.multiple_of(p * B, B), B)

    def top_copy(p, origin):
        part = pl.ds(pl.multiple_of(p * B, B), A_ROWS)
        return pltpu.make_async_copy(origin, raw.at[part], in_sems.at[0, p])

    def deep_copy(p):
        part = pl.ds(pl.multiple_of(p * B + A_ROWS, 8), B - A_ROWS)
        return pltpu.make_async_copy(deep.at[table[5, p]], raw.at[part], in_sems.at[1, p])

    def new_copy(p):
        return pltpu.make_async_copy(new.at[rows(p)], out.at[table[0, p]], out_sems.at[p])

    def dead_copy(p):
        return pltpu.make_async_copy(trailing_in.at[table[0, p]], out.at[table[0, p]], out_sems.at[p])

    def old_copy(p):
        return pltpu.make_async_copy(trailing_in.at[table[0, p]], old.at[rows(p)], in_sems.at[2, p])

    def factor_copies(n):
        block, wide = pl.ds(256 * n, 256), pl.ds(0, 256 * n + 256)
        return [
            pltpu.make_async_copy(a.at[block, wide], b.at[block, wide], sems.at[2 * n + i])
            for i, (a, b) in enumerate(((low_in, low), (high_in, high)))
        ]

    def tile_copy(b):
        return pltpu.make_async_copy(tiles_in.at[b], tiles.at[b], sems.at[8 + b])

    def begin(p, carry):
        deep_copy(p).start()
        for k in range(4):
            @pl.when(table[1, p] == k)
            def _():
                top_copy(p, ring[k - 1].at[table[4, p]] if k else here.at[table[4, p]]).start()
        return carry

    def begin_both(p, carry):
        begin(p, carry)
        old_copy(p).start()
        return carry

    def arrive(c):
        for i in range(2):
            top_copy(2 * c + i, here.at[0]).wait()
            deep_copy(2 * c + i).wait()

    def arrive_old(c):
        for i in range(2):
            old_copy(2 * c + i).wait()

    def solve(c, slot, waits=False):
        block = pl.ds(pl.multiple_of(c * 2 * B, 2 * B), 2 * B)
        for n in range(0, 1024, 256):
            e = n + 256
            if waits:
                for copy in factor_copies(n // 256):
                    copy.wait()
            some = raw[block, :e]
            piece = dot(some, low[n:e, :e], ((1,), (1,))) + dot(some, high[n:e, :e], ((1,), (1,)))
            left[slot, :, n:e] = piece.astype(BF16)

    def subtract(p, slot, first, b):
        for n in range(0, 1024, 256):
            product = dot(left[slot, first * B:, :], tiles[b, n:n + 256, :], ((1,), (1,)))
            for i in range(2 - first):
                before = old[rows(p + i), n:n + 256].astype(F32)
                new[rows(p + i), n:n + 256] = (before - product[i * B:i * B + B, :]).astype(BF16)

    for n in range(4):
        for copy in factor_copies(n):
            copy.start()
        if n == 0:
            lax.fori_loop(0, 2, begin, 0)
    tile_copy(table[2, 0]).start()
    old_copy(0).start()
    old_copy(1).start()
    lax.fori_loop(2, 4, begin_both, 0)
    tile_copy(1 - table[2, 0]).start()
    lax.fori_loop(4, 12, begin_both, 0)
    live = sum(table[3, p] for p in range(12))
    pairs = (live + 1) // 2

    def start_dead(p, carry):
        dead_copy(p).start()
        return carry

    lax.fori_loop(live, 12, start_dead, 0)
    arrive(0)
    solve(0, 0, True)
    tile_copy(0).wait()
    tile_copy(1).wait()
    arrive_old(0)

    def pair(c, carry):
        p = 2 * c

        @pl.when(c < 5)
        def _():
            arrive(c + 1)
            arrive_old(c + 1)

        solve(jnp.minimum(c + 1, 5), lax.rem(c + 1, 2))
        subtract(p, lax.rem(c, 2), 0, table[2, p])
        more = p + 1 < live

        @pl.when(jnp.logical_and(more, table[2, p + 1] != table[2, p]))
        def _():
            subtract(p + 1, lax.rem(c, 2), 1, table[2, p + 1])

        new_copy(p).start()

        @pl.when(more)
        def _():
            new_copy(p + 1).start()

        return carry

    lax.fori_loop(0, pairs, pair, 0)

    def rest(c, carry):
        arrive(c)
        arrive_old(c)
        return carry

    lax.fori_loop(pairs + 1, 6, rest, 0)
    for p in range(12):
        new_copy(p).wait()


def update_slots(table, here, ring, deep, high, low, tiles, trailing):
    hbm = pl.BlockSpec(memory_space=pl.ANY)
    square = pltpu.VMEM((1024, 1024), BF16)
    return pl.pallas_call(
        slot_kernel,
        out_shape=jax.ShapeDtypeStruct((12, B, 1024), BF16),
        in_specs=[pl.BlockSpec(memory_space=pltpu.SMEM)] + [hbm] * 9,
        out_specs=hbm,
        scratch_shapes=[square, square, pltpu.VMEM((2, 1024, 1024), BF16)]
        + [pltpu.VMEM((12 * B, 1024), BF16)] * 3
        + [pltpu.VMEM((2, 2 * B, 1024), BF16), pltpu.SemaphoreType.DMA((3, 12))]
        + [pltpu.SemaphoreType.DMA((12,)), pltpu.SemaphoreType.DMA((10,))],
        compiler_params=pltpu.CompilerParams(vmem_limit_bytes=60 << 20),
        cost_estimate=pl.CostEstimate(flops=8_000_000_000, bytes_accessed=20_000_000, transcendentals=0),
        name="slots",
    )(table, here, *ring, deep, high, low, tiles, trailing)


def pack_kernel(x, odd, source, *outs):
    for i, k in enumerate(ORDER[1:]):
        dest = lax.rem(x[0] + k, 4)
        for z in range(8):
            outs[i][z] = source[z, odd[dest, z]]


def pack(x, odd, source):
    smem, vmem = pl.BlockSpec(memory_space=pltpu.SMEM), pl.BlockSpec(memory_space=pltpu.VMEM)
    return pl.pallas_call(
        pack_kernel,
        out_shape=[jax.ShapeDtypeStruct((8, A_ROWS, 1024), BF16)] * 3,
        in_specs=[smem, smem, vmem],
        out_specs=[vmem] * 3,
        compiler_params=pltpu.CompilerParams(vmem_limit_bytes=4 << 20),
        cost_estimate=pl.CostEstimate(flops=0, bytes_accessed=9_000_000, transcendentals=0),
        name="pack",
    )(x, odd, source)


def shift_x(x, k):
    return lax.ppermute(x, "col", [(c, c // 4 * 4 + (c + k) % 4) for c in range(32)])


def gather_z(x):
    groups = [[4 * z + c for z in range(8)] for c in range(4)]
    return lax.all_gather(x, "col", axis=0, tiled=False, axis_index_groups=groups)


def shift_y(x, k):
    return lax.ppermute(x, "row", [(r, (r + 2 * k) % 8) for r in range(8)])


def other_core(x):
    return lax.ppermute(x, "row", [(r, r ^ 1) for r in range(8)])


def same_core(x):
    return [x] + [shift_y(x, k) for k in ORDER[1:]]


def local(diag_block, panel, trailing, slot_rows, slot_cols):
    row, col = lax.axis_index("row"), lax.axis_index("col")
    z, x = col // 4, col % 4
    order = jnp.array(ORDER, jnp.int32)
    ranks = jnp.concatenate([(row - 2 * order) % 8, ((row ^ 1) - 2 * order) % 8]).astype(jnp.int32)

    upper = lax.optimization_barrier(panel[:, :A_ROWS])
    here = gather_z(upper)
    diag_parts = same_core(diag_block)
    diag_parts += [other_core(p) for p in diag_parts]
    own, lower, diag_parts = lax.optimization_barrier((panel, panel[:, A_ROWS:], diag_parts))
    members = [lower] + [shift_x(lower, k) for k in ORDER[1:]]
    own_parts = [own, shift_y(own, 1), shift_y(own, 3)]

    four = lax.dynamic_index_in_dim(slot_rows.reshape(8, 4, 12), z, 0, keepdims=False)
    wanted = 2 * (4 * jnp.arange(8, dtype=jnp.int32) + x) + 1
    odd = jnp.any(four[:, None, :] == wanted[None, :, None], axis=2).astype(jnp.int32)

    work = first_blocks(ranks, diag_parts)
    members, own_parts, work, own = lax.optimization_barrier((members, own_parts, work, panel))
    deep = gather_z(jnp.stack(members))
    own_parts.append(shift_y(own, 2))
    here, work = lax.optimization_barrier((here, work))
    messages = pack(x.reshape(1), odd, here)
    work, messages = lax.optimization_barrier((work, messages))
    ring = [shift_x(m, k) for m, k in zip(messages, ORDER[1:])]
    high, low = inverse_parts(work)
    own_parts, high, low = lax.optimization_barrier((own_parts, high, low))
    own_parts += [other_core(p) for p in own_parts]
    tiles, panel_factor = solve_own(ranks, own_parts, high, low)

    slot_rows, slot_cols, high, low = lax.optimization_barrier((slot_rows, slot_cols, high, low))
    rows = lax.dynamic_index_in_dim(slot_rows, col, 0, keepdims=False)
    cols = lax.dynamic_index_in_dim(slot_cols, col, 0, keepdims=False)
    live = rows >= 0
    key = jnp.where(live, cols, 2)
    slot = jnp.arange(12, dtype=jnp.int32)
    before = (key[None, :] < key[:, None]) | ((key[None, :] == key[:, None]) & (slot[None, :] < slot[:, None]))
    place = jnp.sum(before.astype(jnp.int32), axis=1)
    tile = jnp.maximum(rows, 0)
    owner_z, apart = tile // 8, (x - tile // 2 % 4) % 4
    member = jnp.where(apart == 3, 2, jnp.where(apart == 2, 3, apart))
    inside = jnp.where(apart == 0, 2 * owner_z + tile % 2, owner_z)
    below = (4 * owner_z + member) * 2 + tile % 2
    fields = jnp.stack([slot, member, cols, live.astype(jnp.int32), inside, below])
    chosen = (place[None, :] == slot[:, None]).astype(jnp.int32)
    table = jnp.sum(fields[:, None, :] * chosen[None, :, :], axis=2)

    here = here.reshape(16, A_ROWS, 1024)
    deep = deep.reshape(64, B - A_ROWS, 1024)
    updated = update_slots(table, here, ring, deep, high, low, tiles, trailing[0])
    return (panel_factor, updated[None])


def solution(mesh):
    return jax.shard_map(
        local,
        mesh=mesh,
        in_specs=(P("row", None), P("col", "row", None), P("col", None, "row", None), P(), P()),
        out_specs=(P("col", "row", None), P("col", None, "row", None)),
        check_vma=False,
    )
```

```python
import functools

import jax
import jax.numpy as jnp
from jax import lax
from jax.experimental import pallas as pl
from jax.experimental.pallas import tpu as pltpu
from jax.sharding import PartitionSpec as P

HIGHEST = lax.Precision.HIGHEST
F32, BF16 = jnp.float32, jnp.bfloat16
B = 128
SPLIT = 1
A_ROWS = 80
ORDER = (0, 1, 3, 2)


def lane_splat(x, lane):
    return jnp.broadcast_to(x[:, lane:lane + 1], (8, B))


def row_splat(x, row):
    return jnp.broadcast_to(x[row:row + 1, :], (8, B))


def tree_sum(terms):
    terms = list(terms)
    while len(terms) > 1:
        terms = [terms[i] + terms[i + 1] for i in range(0, len(terms), 2)]
    return terms[0]


def inverse_factor(block, out):
    sub = lax.broadcasted_iota(jnp.int32, (8, B), 0)
    lane = lax.broadcasted_iota(jnp.int32, (8, B), 1)
    rows = [block[8 * g:8 * g + 8, :] for g in range(16)]
    ones = [jnp.where(lane == sub + 8 * g, 1.0, 0.0).astype(F32) for g in range(16)]
    for g in range(16):
        left, right = rows[g], ones[g]
        cols = [lane_splat(left, 8 * g + k) for k in range(8)]
        done = jnp.zeros((8, B), F32)
        for k in range(8):
            here = sub == k
            pivot = row_splat(cols[k], k)
            recip = 1.0 / pivot
            right_row = row_splat(right, k)
            done = jnp.where(here, right_row * lax.rsqrt(pivot), done)
            left_row = row_splat(left, k) * recip
            right_row = right_row * recip
            for m in range(k + 1, 8):
                entry = row_splat(cols[m], k) * recip
                cols[m] = jnp.where(here, entry, cols[m] - cols[k] * entry)
            left = jnp.where(here, left_row, left - cols[k] * left_row)
            right = jnp.where(here, right_row, right - cols[k] * right_row)
        out[8 * g:8 * g + 8, :] = done
        if g < 15:
            left_rows = [row_splat(left, k) for k in range(8)]
            right_rows = [row_splat(right, k) for k in range(8)]
            for h in range(g + 1, 16):
                coefs = [lane_splat(rows[h], 8 * g + k) for k in range(8)]
                rows[h] = rows[h] - tree_sum(coefs[k] * left_rows[k] for k in range(8))
                ones[h] = ones[h] - tree_sum(coefs[k] * right_rows[k] for k in range(8))


def dot(a, b, contract, precision=None):
    return lax.dot_general(a, b, ((contract[0], contract[1]), ((), ())), precision=precision, preferred_element_type=F32)


def clear_below(work, inv, j):
    s, e = j * B, j * B + B
    if j:
        work[s:e, :s] = dot(inv, work[s:e, :s], ((1,), (0,)), HIGHEST)
    work[s:e, s:e] = inv
    if j < 7:
        work[s:e, e:] = dot(inv, work[s:e, e:], ((1,), (0,)), HIGHEST)
    for t in range(e, 1024, B):
        coef = work[s:e, t:t + B]
        if j:
            work[t:t + B, :s] -= dot(coef, work[s:e, :s], ((0,), (0,)), HIGHEST)
        work[t:t + B, s:e] = -dot(coef, inv, ((0,), (0,)), HIGHEST)
        work[t:t + B, t:] -= dot(coef, work[s:e, t:], ((0,), (0,)), HIGHEST)


def eliminate(work, diag_inverse, first, last):
    def step(j, carry):
        here = pl.ds(pl.multiple_of(j * B, B), B)
        inverse_factor(work[here, here], diag_inverse)
        work[here, :] = dot(diag_inverse[...], work[here, :], ((1,), (0,)), HIGHEST)
        work[here, here] = diag_inverse[...]

        def below(i, carry):
            there = pl.ds(pl.multiple_of(i * B, B), B)
            work[there, here] = jnp.zeros((B, B), F32)
            work[there, :] -= dot(work[here, there], work[here, :], ((0,), (0,)), HIGHEST)
            return carry

        lax.fori_loop(j + 1, 8, below, 0)
        return carry

    lax.fori_loop(first, last, step, 0)


def first_kernel(ranks, *refs):
    parts, work, diag_inverse = refs[:8], refs[8], refs[9]
    for q in range(8):
        work[pl.ds(pl.multiple_of(ranks[q] * B, B), B), :] = parts[q][...]
    inverse_factor(work[:B, :B], diag_inverse)
    clear_below(work, diag_inverse[...], 0)


def second_kernel(start, work, high, low, diag_inverse):
    eliminate(work, diag_inverse, SPLIT, 8)
    for j in range(8):
        s, e = j * B, j * B + B
        whole = work[s:e, :e]
        top = whole.astype(BF16)
        high[s:e, :e] = top
        low[s:e, :e] = (whole - top.astype(F32)).astype(BF16)
        if e < 1024:
            high[s:e, e:] = jnp.zeros((B, 1024 - e), BF16)
            low[s:e, e:] = jnp.zeros((B, 1024 - e), BF16)


def first_blocks(ranks, parts):
    vmem = pl.BlockSpec(memory_space=pltpu.VMEM)
    return pl.pallas_call(
        first_kernel,
        out_shape=jax.ShapeDtypeStruct((1024, 1024), F32),
        in_specs=[pl.BlockSpec(memory_space=pltpu.SMEM)] + [vmem] * 8,
        out_specs=vmem,
        scratch_shapes=[pltpu.VMEM((B, B), F32)],
        compiler_params=pltpu.CompilerParams(vmem_limit_bytes=8 << 20),
        cost_estimate=pl.CostEstimate(flops=20_000_000_000, bytes_accessed=50_000_000, transcendentals=0),
        name="first",
    )(ranks, *parts)


def inverse_parts(work):
    vmem = pl.BlockSpec(memory_space=pltpu.VMEM)
    half = jax.ShapeDtypeStruct((1024, 1024), BF16)
    _, high, low = pl.pallas_call(
        second_kernel,
        out_shape=(jax.ShapeDtypeStruct((1024, 1024), F32), half, half),
        in_specs=[vmem],
        out_specs=(vmem, vmem, vmem),
        scratch_shapes=[pltpu.VMEM((B, B), F32)],
        input_output_aliases={0: 0},
        compiler_params=pltpu.CompilerParams(vmem_limit_bytes=8 << 20),
        cost_estimate=pl.CostEstimate(flops=20_000_000_000, bytes_accessed=50_000_000, transcendentals=0),
        name="second",
    )(work)
    return high, low


def solve_rows(raw, high, low):
    pieces = []
    for n in range(4):
        s, e = 256 * n, 256 * n + 256
        left = raw[:, :e]
        piece = dot(left, low[s:e, :e], ((1,), (1,))) + dot(left, high[s:e, :e], ((1,), (1,)))
        pieces.append(piece.astype(BF16))
    return jnp.concatenate(pieces, axis=1)


def own_kernel(ranks, *refs):
    parts, (high, low, tiles, mine, raw) = refs[:8], refs[8:]
    for q in range(8):
        raw[q] = parts[q][...].reshape(2 * B, 1024)

    def step(q, carry):
        solved = solve_rows(raw[q], high, low).reshape(2, B, 1024)
        tiles[:, pl.ds(pl.multiple_of(ranks[q] * B, B), B), :] = solved
        return carry

    lax.fori_loop(0, 8, step, 0)
    mine[...] = tiles[:, pl.ds(pl.multiple_of(ranks[0] * B, B), B), :]


def solve_own(ranks, parts, high, low):
    vmem = pl.BlockSpec(memory_space=pltpu.VMEM)
    return pl.pallas_call(
        own_kernel,
        out_shape=(jax.ShapeDtypeStruct((2, 1024, 1024), BF16), jax.ShapeDtypeStruct((2, B, 1024), BF16)),
        in_specs=[pl.BlockSpec(memory_space=pltpu.SMEM)] + [vmem] * 10,
        out_specs=(vmem, vmem),
        scratch_shapes=[pltpu.VMEM((8, 2 * B, 1024), BF16)],
        compiler_params=pltpu.CompilerParams(vmem_limit_bytes=10 << 20),
        cost_estimate=pl.CostEstimate(flops=1000, bytes_accessed=1000, transcendentals=0),
        name="own",
    )(ranks, *parts, high, low)


def slot_kernel(table, here, r1, r2, r3, deep, high_in, low_in, tiles_in, trailing_in, out, *scratch):
    high, low, tiles, raw, old, new, left, in_sems, out_sems, sems = scratch
    ring = (r1, r2, r3)

    def rows(p):
        return pl.ds(pl.multiple_of(p * B, B), B)

    def top_copy(p, origin):
        part = pl.ds(pl.multiple_of(p * B, B), A_ROWS)
        return pltpu.make_async_copy(origin, raw.at[part], in_sems.at[0, p])

    def deep_copy(p):
        part = pl.ds(pl.multiple_of(p * B + A_ROWS, 8), B - A_ROWS)
        return pltpu.make_async_copy(deep.at[table[5, p]], raw.at[part], in_sems.at[1, p])

    def new_copy(p):
        return pltpu.make_async_copy(new.at[rows(p)], out.at[table[0, p]], out_sems.at[p])

    def dead_copy(p):
        return pltpu.make_async_copy(old.at[rows(p)], out.at[table[0, p]], out_sems.at[p])

    def old_copy(p):
        return pltpu.make_async_copy(trailing_in.at[table[0, p]], old.at[rows(p)], in_sems.at[2, p])

    def factor_copies(n):
        block, wide = pl.ds(256 * n, 256), pl.ds(0, 256 * n + 256)
        return [
            pltpu.make_async_copy(a.at[block, wide], b.at[block, wide], sems.at[2 * n + i])
            for i, (a, b) in enumerate(((low_in, low), (high_in, high)))
        ]

    def tile_copy(b):
        return pltpu.make_async_copy(tiles_in.at[b], tiles.at[b], sems.at[8 + b])

    def begin(p, carry):
        deep_copy(p).start()
        for k in range(4):
            @pl.when(table[1, p] == k)
            def _():
                top_copy(p, ring[k - 1].at[table[4, p]] if k else here.at[table[4, p]]).start()
        return carry

    def begin_both(p, carry):
        begin(p, carry)
        old_copy(p).start()
        return carry

    def arrive(c):
        for i in range(2):
            top_copy(2 * c + i, here.at[0]).wait()
            deep_copy(2 * c + i).wait()

    def arrive_old(c):
        for i in range(2):
            old_copy(2 * c + i).wait()

    def solve(c, slot, waits=False):
        block = pl.ds(pl.multiple_of(c * 2 * B, 2 * B), 2 * B)
        for n in range(0, 1024, 256):
            e = n + 256
            if waits:
                for copy in factor_copies(n // 256):
                    copy.wait()
            some = raw[block, :e]
            piece = dot(some, low[n:e, :e], ((1,), (1,))) + dot(some, high[n:e, :e], ((1,), (1,)))
            left[slot, :, n:e] = piece.astype(BF16)

    def subtract(p, slot, first, b):
        for n in range(0, 1024, 256):
            product = dot(left[slot, first * B:, :], tiles[b, n:n + 256, :], ((1,), (1,)))
            for i in range(2 - first):
                before = old[rows(p + i), n:n + 256].astype(F32)
                new[rows(p + i), n:n + 256] = (before - product[i * B:i * B + B, :]).astype(BF16)

    for n in range(4):
        for copy in factor_copies(n):
            copy.start()
        if n == 0:
            lax.fori_loop(0, 2, begin, 0)
    tile_copy(table[2, 0]).start()
    old_copy(0).start()
    old_copy(1).start()
    lax.fori_loop(2, 4, begin_both, 0)
    tile_copy(1 - table[2, 0]).start()
    lax.fori_loop(4, 12, begin_both, 0)
    live = sum(table[3, p] for p in range(12))
    pairs = (live + 1) // 2

    arrive(0)
    solve(0, 0, True)
    tile_copy(0).wait()
    tile_copy(1).wait()
    arrive_old(0)

    def pair(c, carry):
        p = 2 * c

        @pl.when(c < 5)
        def _():
            arrive(c + 1)
            arrive_old(c + 1)

        solve(jnp.minimum(c + 1, 5), lax.rem(c + 1, 2))
        subtract(p, lax.rem(c, 2), 0, table[2, p])
        more = p + 1 < live

        @pl.when(jnp.logical_and(more, table[2, p + 1] != table[2, p]))
        def _():
            subtract(p + 1, lax.rem(c, 2), 1, table[2, p + 1])

        new_copy(p).start()

        @pl.when(more)
        def _():
            new_copy(p + 1).start()

        return carry

    lax.fori_loop(0, pairs, pair, 0)

    def rest(c, carry):
        arrive(c)
        arrive_old(c)
        return carry

    def start_dead(p, carry):
        dead_copy(p).start()
        return carry

    lax.fori_loop(pairs + 1, 6, rest, 0)
    lax.fori_loop(live, 12, start_dead, 0)
    for p in range(12):
        new_copy(p).wait()


def update_slots(table, here, ring, deep, high, low, tiles, trailing):
    hbm = pl.BlockSpec(memory_space=pl.ANY)
    square = pltpu.VMEM((1024, 1024), BF16)
    return pl.pallas_call(
        slot_kernel,
        out_shape=jax.ShapeDtypeStruct((12, B, 1024), BF16),
        in_specs=[pl.BlockSpec(memory_space=pltpu.SMEM)] + [hbm] * 9,
        out_specs=hbm,
        scratch_shapes=[square, square, pltpu.VMEM((2, 1024, 1024), BF16)]
        + [pltpu.VMEM((12 * B, 1024), BF16)] * 3
        + [pltpu.VMEM((2, 2 * B, 1024), BF16), pltpu.SemaphoreType.DMA((3, 12))]
        + [pltpu.SemaphoreType.DMA((12,)), pltpu.SemaphoreType.DMA((10,))],
        compiler_params=pltpu.CompilerParams(vmem_limit_bytes=60 << 20),
        cost_estimate=pl.CostEstimate(flops=8_000_000_000, bytes_accessed=20_000_000, transcendentals=0),
        name="slots",
    )(table, here, *ring, deep, high, low, tiles, trailing)


def pack_kernel(x, odd, source, *outs):
    for i, k in enumerate(ORDER[1:]):
        dest = lax.rem(x[0] + k, 4)
        for z in range(8):
            outs[i][z] = source[z, odd[dest, z]]


def pack(x, odd, source):
    smem, vmem = pl.BlockSpec(memory_space=pltpu.SMEM), pl.BlockSpec(memory_space=pltpu.VMEM)
    return pl.pallas_call(
        pack_kernel,
        out_shape=[jax.ShapeDtypeStruct((8, A_ROWS, 1024), BF16)] * 3,
        in_specs=[smem, smem, vmem],
        out_specs=[vmem] * 3,
        compiler_params=pltpu.CompilerParams(vmem_limit_bytes=4 << 20),
        cost_estimate=pl.CostEstimate(flops=0, bytes_accessed=9_000_000, transcendentals=0),
        name="pack",
    )(x, odd, source)


def shift_x(x, k):
    return lax.ppermute(x, "col", [(c, c // 4 * 4 + (c + k) % 4) for c in range(32)])


def gather_z(x):
    groups = [[4 * z + c for z in range(8)] for c in range(4)]
    return lax.all_gather(x, "col", axis=0, tiled=False, axis_index_groups=groups)


def shift_y(x, k):
    return lax.ppermute(x, "row", [(r, (r + 2 * k) % 8) for r in range(8)])


def other_core(x):
    return lax.ppermute(x, "row", [(r, r ^ 1) for r in range(8)])


def same_core(x):
    return [x] + [shift_y(x, k) for k in ORDER[1:]]


def local(diag_block, panel, trailing, slot_rows, slot_cols):
    row, col = lax.axis_index("row"), lax.axis_index("col")
    z, x = col // 4, col % 4
    order = jnp.array(ORDER, jnp.int32)
    ranks = jnp.concatenate([(row - 2 * order) % 8, ((row ^ 1) - 2 * order) % 8]).astype(jnp.int32)

    upper = lax.optimization_barrier(panel[:, :A_ROWS])
    here = gather_z(upper)
    diag_parts = same_core(diag_block)
    diag_parts += [other_core(p) for p in diag_parts]
    own, lower, diag_parts = lax.optimization_barrier((panel, panel[:, A_ROWS:], diag_parts))
    members = [lower] + [shift_x(lower, k) for k in ORDER[1:]]
    own_parts = [own, shift_y(own, 1), shift_y(own, 3)]

    four = lax.dynamic_index_in_dim(slot_rows.reshape(8, 4, 12), z, 0, keepdims=False)
    wanted = 2 * (4 * jnp.arange(8, dtype=jnp.int32) + x) + 1
    odd = jnp.any(four[:, None, :] == wanted[None, :, None], axis=2).astype(jnp.int32)

    work = first_blocks(ranks, diag_parts)
    members, own_parts, work, own = lax.optimization_barrier((members, own_parts, work, panel))
    deep = gather_z(jnp.stack(members))
    own_parts.append(shift_y(own, 2))
    here, work = lax.optimization_barrier((here, work))
    messages = pack(x.reshape(1), odd, here)
    work, messages = lax.optimization_barrier((work, messages))
    ring = [shift_x(m, k) for m, k in zip(messages, ORDER[1:])]
    high, low = inverse_parts(work)
    own_parts, high, low = lax.optimization_barrier((own_parts, high, low))
    own_parts += [other_core(p) for p in own_parts]
    tiles, panel_factor = solve_own(ranks, own_parts, high, low)

    slot_rows, slot_cols, high, low = lax.optimization_barrier((slot_rows, slot_cols, high, low))
    rows = lax.dynamic_index_in_dim(slot_rows, col, 0, keepdims=False)
    cols = lax.dynamic_index_in_dim(slot_cols, col, 0, keepdims=False)
    live = rows >= 0
    key = jnp.where(live, cols, 2)
    slot = jnp.arange(12, dtype=jnp.int32)
    before = (key[None, :] < key[:, None]) | ((key[None, :] == key[:, None]) & (slot[None, :] < slot[:, None]))
    place = jnp.sum(before.astype(jnp.int32), axis=1)
    tile = jnp.maximum(rows, 0)
    owner_z, apart = tile // 8, (x - tile // 2 % 4) % 4
    member = jnp.where(apart == 3, 2, jnp.where(apart == 2, 3, apart))
    inside = jnp.where(apart == 0, 2 * owner_z + tile % 2, owner_z)
    below = (4 * owner_z + member) * 2 + tile % 2
    fields = jnp.stack([slot, member, cols, live.astype(jnp.int32), inside, below])
    chosen = (place[None, :] == slot[:, None]).astype(jnp.int32)
    table = jnp.sum(fields[:, None, :] * chosen[None, :, :], axis=2)

    here = here.reshape(16, A_ROWS, 1024)
    deep = deep.reshape(64, B - A_ROWS, 1024)
    updated = update_slots(table, here, ring, deep, high, low, tiles, trailing[0])
    return (panel_factor, updated[None])


def solution(mesh):
    return jax.shard_map(
        local,
        mesh=mesh,
        in_specs=(P("row", None), P("col", "row", None), P("col", None, "row", None), P(), P()),
        out_specs=(P("col", "row", None), P("col", None, "row", None)),
        check_vma=False,
    )
```

```python
import functools

import jax
import jax.numpy as jnp
from jax import lax
from jax.experimental import pallas as pl
from jax.experimental.pallas import tpu as pltpu
from jax.sharding import PartitionSpec as P

HIGHEST = lax.Precision.HIGHEST
F32, BF16 = jnp.float32, jnp.bfloat16
B = 128
SPLIT = 1
A_ROWS = 80
ORDER = (0, 1, 3, 2)


def lane_splat(x, lane):
    return jnp.broadcast_to(x[:, lane:lane + 1], (8, B))


def row_splat(x, row):
    return jnp.broadcast_to(x[row:row + 1, :], (8, B))


def tree_sum(terms):
    terms = list(terms)
    while len(terms) > 1:
        terms = [terms[i] + terms[i + 1] for i in range(0, len(terms), 2)]
    return terms[0]


def inverse_factor(block, out):
    sub = lax.broadcasted_iota(jnp.int32, (8, B), 0)
    lane = lax.broadcasted_iota(jnp.int32, (8, B), 1)
    rows = [block[8 * g:8 * g + 8, :] for g in range(16)]
    ones = [jnp.where(lane == sub + 8 * g, 1.0, 0.0).astype(F32) for g in range(16)]
    for g in range(16):
        left, right = rows[g], ones[g]
        cols = [lane_splat(left, 8 * g + k) for k in range(8)]
        done = jnp.zeros((8, B), F32)
        for k in range(8):
            here = sub == k
            pivot = row_splat(cols[k], k)
            recip = 1.0 / pivot
            right_row = row_splat(right, k)
            done = jnp.where(here, right_row * lax.rsqrt(pivot), done)
            left_row = row_splat(left, k) * recip
            right_row = right_row * recip
            for m in range(k + 1, 8):
                entry = row_splat(cols[m], k) * recip
                cols[m] = jnp.where(here, entry, cols[m] - cols[k] * entry)
            left = jnp.where(here, left_row, left - cols[k] * left_row)
            right = jnp.where(here, right_row, right - cols[k] * right_row)
        out[8 * g:8 * g + 8, :] = done
        if g < 15:
            left_rows = [row_splat(left, k) for k in range(8)]
            right_rows = [row_splat(right, k) for k in range(8)]
            for h in range(g + 1, 16):
                coefs = [lane_splat(rows[h], 8 * g + k) for k in range(8)]
                rows[h] = rows[h] - tree_sum(coefs[k] * left_rows[k] for k in range(8))
                ones[h] = ones[h] - tree_sum(coefs[k] * right_rows[k] for k in range(8))


def dot(a, b, contract, precision=None):
    return lax.dot_general(a, b, ((contract[0], contract[1]), ((), ())), precision=precision, preferred_element_type=F32)


def clear_below(work, inv, j):
    s, e = j * B, j * B + B
    if j:
        work[s:e, :s] = dot(inv, work[s:e, :s], ((1,), (0,)), HIGHEST)
    work[s:e, s:e] = inv
    if j < 7:
        work[s:e, e:] = dot(inv, work[s:e, e:], ((1,), (0,)), HIGHEST)
    for t in range(e, 1024, B):
        coef = work[s:e, t:t + B]
        if j:
            work[t:t + B, :s] -= dot(coef, work[s:e, :s], ((0,), (0,)), HIGHEST)
        work[t:t + B, s:e] = -dot(coef, inv, ((0,), (0,)), HIGHEST)
        work[t:t + B, t:] -= dot(coef, work[s:e, t:], ((0,), (0,)), HIGHEST)


def eliminate(work, diag_inverse, first, last):
    def step(j, carry):
        here = pl.ds(pl.multiple_of(j * B, B), B)
        inverse_factor(work[here, here], diag_inverse)
        branches = [functools.partial(clear_below, work, diag_inverse[...], k) for k in range(first, last)]
        lax.switch(j - first, branches)
        return carry

    lax.fori_loop(first, last, step, 0)


def first_kernel(ranks, *refs):
    parts, work, diag_inverse = refs[:8], refs[8], refs[9]
    for q in range(8):
        work[pl.ds(pl.multiple_of(ranks[q] * B, B), B), :] = parts[q][...]
    inverse_factor(work[:B, :B], diag_inverse)
    clear_below(work, diag_inverse[...], 0)


def second_kernel(start, work, high, low, diag_inverse):
    eliminate(work, diag_inverse, SPLIT, 8)
    for j in range(8):
        s, e = j * B, j * B + B
        whole = work[s:e, :e]
        top = whole.astype(BF16)
        high[s:e, :e] = top
        low[s:e, :e] = (whole - top.astype(F32)).astype(BF16)
        if e < 1024:
            high[s:e, e:] = jnp.zeros((B, 1024 - e), BF16)
            low[s:e, e:] = jnp.zeros((B, 1024 - e), BF16)


def first_blocks(ranks, parts):
    vmem = pl.BlockSpec(memory_space=pltpu.VMEM)
    return pl.pallas_call(
        first_kernel,
        out_shape=jax.ShapeDtypeStruct((1024, 1024), F32),
        in_specs=[pl.BlockSpec(memory_space=pltpu.SMEM)] + [vmem] * 8,
        out_specs=vmem,
        scratch_shapes=[pltpu.VMEM((B, B), F32)],
        compiler_params=pltpu.CompilerParams(vmem_limit_bytes=8 << 20),
        cost_estimate=pl.CostEstimate(flops=20_000_000_000, bytes_accessed=50_000_000, transcendentals=0),
        name="first",
    )(ranks, *parts)


def inverse_parts(work):
    vmem = pl.BlockSpec(memory_space=pltpu.VMEM)
    half = jax.ShapeDtypeStruct((1024, 1024), BF16)
    _, high, low = pl.pallas_call(
        second_kernel,
        out_shape=(jax.ShapeDtypeStruct((1024, 1024), F32), half, half),
        in_specs=[vmem],
        out_specs=(vmem, vmem, vmem),
        scratch_shapes=[pltpu.VMEM((B, B), F32)],
        input_output_aliases={0: 0},
        compiler_params=pltpu.CompilerParams(vmem_limit_bytes=8 << 20),
        cost_estimate=pl.CostEstimate(flops=20_000_000_000, bytes_accessed=50_000_000, transcendentals=0),
        name="second",
    )(work)
    return high, low


def solve_rows(raw, high, low):
    pieces = []
    for n in range(4):
        s, e = 256 * n, 256 * n + 256
        left = raw[:, :e]
        piece = dot(left, low[s:e, :e], ((1,), (1,))) + dot(left, high[s:e, :e], ((1,), (1,)))
        pieces.append(piece.astype(BF16))
    return jnp.concatenate(pieces, axis=1)


def own_kernel(ranks, *refs):
    parts, (high, low, tiles, mine, raw) = refs[:8], refs[8:]
    for q in range(8):
        raw[q] = parts[q][...].reshape(2 * B, 1024)

    def step(q, carry):
        solved = solve_rows(raw[q], high, low).reshape(2, B, 1024)
        tiles[:, pl.ds(pl.multiple_of(ranks[q] * B, B), B), :] = solved
        return carry

    lax.fori_loop(0, 8, step, 0)
    mine[...] = tiles[:, pl.ds(pl.multiple_of(ranks[0] * B, B), B), :]


def solve_own(ranks, parts, high, low):
    vmem = pl.BlockSpec(memory_space=pltpu.VMEM)
    return pl.pallas_call(
        own_kernel,
        out_shape=(jax.ShapeDtypeStruct((2, 1024, 1024), BF16), jax.ShapeDtypeStruct((2, B, 1024), BF16)),
        in_specs=[pl.BlockSpec(memory_space=pltpu.SMEM)] + [vmem] * 10,
        out_specs=(vmem, vmem),
        scratch_shapes=[pltpu.VMEM((8, 2 * B, 1024), BF16)],
        compiler_params=pltpu.CompilerParams(vmem_limit_bytes=10 << 20),
        cost_estimate=pl.CostEstimate(flops=1000, bytes_accessed=1000, transcendentals=0),
        name="own",
    )(ranks, *parts, high, low)


def slot_kernel(table, here, r1, r2, r3, deep, high_in, low_in, tiles_in, trailing_in, out, *scratch):
    high, low, tiles, raw, old, new, left, in_sems, out_sems, sems = scratch
    ring = (r1, r2, r3)

    def rows(p):
        return pl.ds(pl.multiple_of(p * B, B), B)

    def top_copy(p, origin):
        part = pl.ds(pl.multiple_of(p * B, B), A_ROWS)
        return pltpu.make_async_copy(origin, raw.at[part], in_sems.at[0, p])

    def deep_copy(p):
        part = pl.ds(pl.multiple_of(p * B + A_ROWS, 8), B - A_ROWS)
        return pltpu.make_async_copy(deep.at[table[5, p]], raw.at[part], in_sems.at[1, p])

    def new_copy(p):
        return pltpu.make_async_copy(new.at[rows(p)], out.at[table[0, p]], out_sems.at[p])

    def dead_copy(p):
        return pltpu.make_async_copy(old.at[rows(p)], out.at[table[0, p]], out_sems.at[p])

    def old_copy(p):
        return pltpu.make_async_copy(trailing_in.at[table[0, p]], old.at[rows(p)], in_sems.at[2, p])

    def factor_copies(n):
        block, wide = pl.ds(256 * n, 256), pl.ds(0, 256 * n + 256)
        return [
            pltpu.make_async_copy(a.at[block, wide], b.at[block, wide], sems.at[2 * n + i])
            for i, (a, b) in enumerate(((low_in, low), (high_in, high)))
        ]

    def tile_copy(b):
        return pltpu.make_async_copy(tiles_in.at[b], tiles.at[b], sems.at[8 + b])

    def begin(p, carry):
        deep_copy(p).start()
        for k in range(4):
            @pl.when(table[1, p] == k)
            def _():
                top_copy(p, ring[k - 1].at[table[4, p]] if k else here.at[table[4, p]]).start()
        return carry

    def begin_both(p, carry):
        begin(p, carry)
        old_copy(p).start()
        return carry

    def arrive(c):
        for i in range(2):
            top_copy(2 * c + i, here.at[0]).wait()
            deep_copy(2 * c + i).wait()

    def arrive_old(c):
        for i in range(2):
            old_copy(2 * c + i).wait()

    def solve(c, slot, waits=False):
        block = pl.ds(pl.multiple_of(c * 2 * B, 2 * B), 2 * B)
        for n in range(0, 1024, 256):
            e = n + 256
            if waits:
                for copy in factor_copies(n // 256):
                    copy.wait()
            some = raw[block, :e]
            piece = dot(some, low[n:e, :e], ((1,), (1,))) + dot(some, high[n:e, :e], ((1,), (1,)))
            left[slot, :, n:e] = piece.astype(BF16)

    def subtract(p, slot, first, b):
        for n in range(0, 1024, 256):
            product = dot(left[slot, first * B:, :], tiles[b, n:n + 256, :], ((1,), (1,)))
            for i in range(2 - first):
                before = old[rows(p + i), n:n + 256].astype(F32)
                new[rows(p + i), n:n + 256] = (before - product[i * B:i * B + B, :]).astype(BF16)

    for n in range(4):
        for copy in factor_copies(n):
            copy.start()
        if n == 0:
            lax.fori_loop(0, 2, begin, 0)
    tile_copy(table[2, 0]).start()
    old_copy(0).start()
    old_copy(1).start()
    lax.fori_loop(2, 4, begin_both, 0)
    tile_copy(1 - table[2, 0]).start()
    lax.fori_loop(4, 12, begin_both, 0)
    live = sum(table[3, p] for p in range(12))
    pairs = (live + 1) // 2

    arrive(0)
    solve(0, 0, True)
    tile_copy(0).wait()
    tile_copy(1).wait()
    arrive_old(0)

    def pair(c, carry):
        p = 2 * c

        @pl.when(c < 5)
        def _():
            arrive(c + 1)
            arrive_old(c + 1)

        solve(jnp.minimum(c + 1, 5), lax.rem(c + 1, 2))
        subtract(p, lax.rem(c, 2), 0, table[2, p])
        more = p + 1 < live

        @pl.when(jnp.logical_and(more, table[2, p + 1] != table[2, p]))
        def _():
            subtract(p + 1, lax.rem(c, 2), 1, table[2, p + 1])

        new_copy(p).start()

        @pl.when(more)
        def _():
            new_copy(p + 1).start()

        return carry

    lax.fori_loop(0, pairs, pair, 0)

    def rest(c, carry):
        arrive(c)
        arrive_old(c)
        return carry

    def start_dead(p, carry):
        dead_copy(p).start()
        return carry

    lax.fori_loop(pairs + 1, 6, rest, 0)
    lax.fori_loop(live, 12, start_dead, 0)
    for p in range(12):
        new_copy(p).wait()


def update_slots(table, here, ring, deep, high, low, tiles, trailing):
    hbm = pl.BlockSpec(memory_space=pl.ANY)
    square = pltpu.VMEM((1024, 1024), BF16)
    return pl.pallas_call(
        slot_kernel,
        out_shape=jax.ShapeDtypeStruct((12, B, 1024), BF16),
        in_specs=[pl.BlockSpec(memory_space=pltpu.SMEM)] + [hbm] * 9,
        out_specs=hbm,
        scratch_shapes=[square, square, pltpu.VMEM((2, 1024, 1024), BF16)]
        + [pltpu.VMEM((12 * B, 1024), BF16)] * 3
        + [pltpu.VMEM((2, 2 * B, 1024), BF16), pltpu.SemaphoreType.DMA((3, 12))]
        + [pltpu.SemaphoreType.DMA((12,)), pltpu.SemaphoreType.DMA((10,))],
        compiler_params=pltpu.CompilerParams(vmem_limit_bytes=60 << 20),
        cost_estimate=pl.CostEstimate(flops=8_000_000_000, bytes_accessed=20_000_000, transcendentals=0),
        name="slots",
    )(table, here, *ring, deep, high, low, tiles, trailing)


def pack_kernel(x, odd, source, *outs):
    for i, k in enumerate(ORDER[1:]):
        dest = lax.rem(x[0] + k, 4)
        for z in range(8):
            outs[i][z] = source[z, odd[dest, z]]


def pack(x, odd, source):
    smem, vmem = pl.BlockSpec(memory_space=pltpu.SMEM), pl.BlockSpec(memory_space=pltpu.VMEM)
    return pl.pallas_call(
        pack_kernel,
        out_shape=[jax.ShapeDtypeStruct((8, A_ROWS, 1024), BF16)] * 3,
        in_specs=[smem, smem, vmem],
        out_specs=[vmem] * 3,
        compiler_params=pltpu.CompilerParams(vmem_limit_bytes=4 << 20),
        cost_estimate=pl.CostEstimate(flops=0, bytes_accessed=9_000_000, transcendentals=0),
        name="pack",
    )(x, odd, source)


def shift_x(x, k):
    return lax.ppermute(x, "col", [(c, c // 4 * 4 + (c + k) % 4) for c in range(32)])


def gather_z(x):
    groups = [[4 * z + c for z in range(8)] for c in range(4)]
    return lax.all_gather(x, "col", axis=0, tiled=False, axis_index_groups=groups)


def shift_y(x, k):
    return lax.ppermute(x, "row", [(r, (r + 2 * k) % 8) for r in range(8)])


def other_core(x):
    return lax.ppermute(x, "row", [(r, r ^ 1) for r in range(8)])


def same_core(x):
    return [x] + [shift_y(x, k) for k in ORDER[1:]]


def local(diag_block, panel, trailing, slot_rows, slot_cols):
    row, col = lax.axis_index("row"), lax.axis_index("col")
    z, x = col // 4, col % 4
    order = jnp.array(ORDER, jnp.int32)
    ranks = jnp.concatenate([(row - 2 * order) % 8, ((row ^ 1) - 2 * order) % 8]).astype(jnp.int32)

    upper = lax.optimization_barrier(panel[:, :A_ROWS])
    here = gather_z(upper)
    diag_parts = same_core(diag_block)
    diag_parts += [other_core(p) for p in diag_parts]
    own, lower, diag_parts = lax.optimization_barrier((panel, panel[:, A_ROWS:], diag_parts))
    members = [lower] + [shift_x(lower, k) for k in ORDER[1:]]
    own_parts = [own, shift_y(own, 1), shift_y(own, 3)]

    four = lax.dynamic_index_in_dim(slot_rows.reshape(8, 4, 12), z, 0, keepdims=False)
    wanted = 2 * (4 * jnp.arange(8, dtype=jnp.int32) + x) + 1
    odd = jnp.any(four[:, None, :] == wanted[None, :, None], axis=2).astype(jnp.int32)

    work = first_blocks(ranks, diag_parts)
    members, own_parts, work, own = lax.optimization_barrier((members, own_parts, work, panel))
    deep = gather_z(jnp.stack(members))
    own_parts.append(shift_y(own, 2))
    here, work = lax.optimization_barrier((here, work))
    messages = pack(x.reshape(1), odd, here)
    work, messages = lax.optimization_barrier((work, messages))
    ring = [shift_x(m, k) for m, k in zip(messages, ORDER[1:])]
    high, low = inverse_parts(work)
    own_parts, high, low = lax.optimization_barrier((own_parts, high, low))
    own_parts += [other_core(p) for p in own_parts]
    tiles, panel_factor = solve_own(ranks, own_parts, high, low)

    slot_rows, slot_cols, high, low = lax.optimization_barrier((slot_rows, slot_cols, high, low))
    rows = lax.dynamic_index_in_dim(slot_rows, col, 0, keepdims=False)
    cols = lax.dynamic_index_in_dim(slot_cols, col, 0, keepdims=False)
    live = rows >= 0
    key = jnp.where(live, cols, 2)
    slot = jnp.arange(12, dtype=jnp.int32)
    before = (key[None, :] < key[:, None]) | ((key[None, :] == key[:, None]) & (slot[None, :] < slot[:, None]))
    place = jnp.sum(before.astype(jnp.int32), axis=1)
    tile = jnp.maximum(rows, 0)
    owner_z, apart = tile // 8, (x - tile // 2 % 4) % 4
    member = jnp.where(apart == 3, 2, jnp.where(apart == 2, 3, apart))
    inside = jnp.where(apart == 0, 2 * owner_z + tile % 2, owner_z)
    below = (4 * owner_z + member) * 2 + tile % 2
    fields = jnp.stack([slot, member, cols, live.astype(jnp.int32), inside, below])
    chosen = (place[None, :] == slot[:, None]).astype(jnp.int32)
    table = jnp.sum(fields[:, None, :] * chosen[None, :, :], axis=2)

    here = here.reshape(16, A_ROWS, 1024)
    deep = deep.reshape(64, B - A_ROWS, 1024)
    updated = update_slots(table, here, ring, deep, high, low, tiles, trailing[0])
    return (panel_factor, updated[None])


def solution(mesh):
    return jax.shard_map(
        local,
        mesh=mesh,
        in_specs=(P("row", None), P("col", "row", None), P("col", None, "row", None), P(), P()),
        out_specs=(P("col", "row", None), P("col", None, "row", None)),
        check_vma=False,
    )
```
